32 devices in a mesh: expert: 8 (over z, x), tensor: 4 (over y, core).
Axes of the slice: x: 2, y: 2, z: 4, core: 2. Of those that a mesh axis runs over, the one named last changes fastest.
Arguments:
- tokens: bfloat16 [512, 8192], P('expert', 'tensor'), may hold values from -6 to 6
- frozen_gate_weight: bfloat16 [8192, 28672], P('tensor', 'expert'), may hold values from -0.0625 to 0.0625
- frozen_up_weight: bfloat16 [8192, 28672], P('tensor', 'expert'), may hold values from -0.0625 to 0.0625
- frozen_down_weight: bfloat16 [28672, 8192], P('expert', 'tensor'), may hold values from -0.03125 to 0.03125
- adapter_down_weight: bfloat16 [32, 8192, 128], P('expert', 'tensor'), may hold values from -0.0625 to 0.0625
- adapter_up_weight: bfloat16 [32, 128, 8192], P('expert', None, 'tensor'), may hold values from -0.0625 to 0.0625
- routes: int32 [512, 2], P('expert'), may hold values from 0 to 31, all different within a row; in each aligned block of 64 rows (0 to 63, 64 to 127, ...) at most 8 rows name the same one
- route_gate_weights: float32 [512, 2], P('expert'), may hold values from 0.1 to 1
- output_gradient: bfloat16 [512, 8192], P('expert', 'tensor'), may hold values from -6 to 6
Outputs:
- ffn_out: bfloat16 [512, 8192], P('expert', 'tensor')
- grad_down: bfloat16 [32, 8192, 128], P('expert', 'tensor')
- grad_up: bfloat16 [32, 128, 8192], P('expert', None, 'tensor')
The draws below stay inside these ranges and needn't reach their ends.
Inputs may be any that keep to these rules, and one draw needn't show every extreme that they name: `routes`: the two experts of a token differ. Among the 64 rows of one index of expert no expert is named more than 8 times, and in some such rows one expert is named exactly 8 times.
All inputs are finite; a program needn't handle non-finite values.
Results may differ from the reference program's by a relative error of at most 0.025.
Values may be sent and summed in bfloat16 or wider, within the bound.
A program may use at most 128 MiB of HBM per device.

```python
import math
import jax
import jax.numpy as jnp
import numpy as np
from jax import lax

MODEL_WIDTH = 8192
FF = 28672
ADAPTER_RANK = 128
TOK_DEV = 64
EXPERT_COUNT = 32
MOST = 8
TOKENS = 512
N_EXPERT = 8
N_TENSOR = 4


def steps_of(key, shape, split, low, top_value):
    def one(dim, parts):
        heights = jax.random.uniform(jax.random.fold_in(jax.random.fold_in(key, 6), dim), (parts,), jnp.float32, low / len(split), top_value / len(split))
        return jnp.repeat(jnp.exp(heights), shape[dim] // parts).reshape((-1,) + (1,) * (len(shape) - dim - 1))

    level = one(*split[0])
    for cut in split[1:]:
        level = level * one(*cut)
    return level


def deal_out(stream_key, own, number, rows, amount, top, bound, skew):
    sequence = jax.random.permutation(stream_key, amount)
    crowded, common = portions_of(amount, rows * top, bound, skew, True), portions_of(amount, rows * top, bound, skew, False)
    places = jnp.arange(amount)

    def named(sizes, rotation):
        used = int((sizes > 0).sum())
        fixed = max(1, used // 4)
        moved = fixed + (places - fixed + rotation * (used - fixed)) % max(1, amount - fixed)
        return jnp.zeros((amount,), jnp.int32).at[sequence[jnp.where(places < fixed, places, moved)]].set(jnp.asarray(sizes, jnp.int32))

    sizes = jnp.where(number % 4 == 0, named(crowded, number // 4), named(common, number - number // 4 - 1))
    mixed = jax.random.permutation(jax.random.fold_in(own, 3), amount)
    donor, receiver = mixed[0:amount // 2 * 2:2], mixed[1:amount // 2 * 2:2]
    slack = jnp.minimum(sizes[donor] - 1, bound - sizes[receiver]) // 2
    slack = jnp.where((donor == sequence[0]) | (receiver == sequence[0]) | (sizes[receiver] == 0), 0, jnp.maximum(slack, 0))
    moved = jax.random.randint(jax.random.fold_in(own, 4), (amount // 2,), 0, 1 << 20) % (slack + 1)
    sizes = sizes.at[donor].add(-moved).at[receiver].add(moved)
    labels = jnp.searchsorted(jnp.cumsum(sizes), jnp.arange(rows * top), side="right").astype(jnp.int32)
    grid = labels.reshape(top, rows).T
    grid = grid[jax.random.permutation(jax.random.fold_in(own, 1), rows)]
    rotation = jax.random.randint(jax.random.fold_in(own, 2), (rows, 1), 0, top)
    return jnp.take_along_axis(grid, (jnp.arange(top)[None, :] + rotation) % top, axis=1)


def portions_of(amount, total, most, skew, full):
    loads = [(1 << 20) // math.isqrt(standing ** skew) + 1 for standing in range(1, amount + 1)]
    largest = most if full else min(most, max(-(-total // amount), total * loads[0] // sum(loads)))
    least = 1 if total - largest >= amount - 1 else 0
    counts, rest = [largest] + [least] * (amount - 1), total - largest - least * (amount - 1)
    while rest > 0:
        free = [i for i in range(1, amount) if counts[i] < largest] or [i for i in range(1, amount) if counts[i] < most]
        whole, left = sum([loads[i] for i in free]), rest
        for i in free:
            extra = min(most - counts[i], max(1, left * loads[i] // whole), rest)
            counts[i] = counts[i] + extra
            rest = rest - extra
    return np.array(counts)


def scatter_about(rng, dims, scale, most, split=(), kind=jnp.bfloat16):
    factor_of = steps_of(rng, dims, split, -0.22, 0.18) if split else 1.0
    values = jax.random.normal(rng, dims, jnp.float32) * scale * factor_of
    return jnp.minimum(jnp.maximum(values, -most), most).astype(kind)


def setup_inputs(seed: int = 0) -> dict:
    splits = jax.random.split(jax.random.key(seed), 10)
    tokens = scatter_about(splits[0], (TOKENS, MODEL_WIDTH), 1.0, 6.0, ((0, 8), (1, 4)))
    frozen_gate_weight = scatter_about(splits[1], (MODEL_WIDTH, FF), MODEL_WIDTH ** -0.5, 0.0625, ((0, 4), (1, 8)))
    frozen_up_weight = scatter_about(splits[2], (MODEL_WIDTH, FF), MODEL_WIDTH ** -0.5, 0.0625, ((0, 4), (1, 8)))
    frozen_down_weight = scatter_about(splits[3], (FF, MODEL_WIDTH), FF ** -0.5, 0.03125, ((0, 8), (1, 4)))
    adapter_down_weight = scatter_about(splits[4], (EXPERT_COUNT, MODEL_WIDTH, ADAPTER_RANK), MODEL_WIDTH ** -0.5, 0.0625, ((0, 8), (1, 4)))
    adapter_up_weight = scatter_about(splits[5], (EXPERT_COUNT, ADAPTER_RANK, MODEL_WIDTH), MODEL_WIDTH ** -0.5, 0.0625, ((0, 8), (2, 4)))
    routes_keys = jax.random.split(jax.random.fold_in(splits[6], 1), TOKENS // TOK_DEV)
    routes_turns = jax.random.permutation(jax.random.fold_in(splits[6], 3), TOKENS // TOK_DEV)
    routes = jax.vmap(lambda own, number: deal_out(jax.random.fold_in(splits[6], 2), own, number, TOK_DEV, EXPERT_COUNT, 2, MOST, 2))(routes_keys, routes_turns).reshape((TOKENS, 2))
    route_gate_weights = jnp.clip(0.1 + 0.9 * jax.random.uniform(splits[7], (TOKENS, 2), jnp.float32) ** steps_of(splits[7], (TOKENS, 2), ((0, 8),), -0.2, 0.2), 0.1, 1.0)
    output_gradient = scatter_about(splits[8], (TOKENS, MODEL_WIDTH), 1.0, 6.0, ((0, 8), (1, 4)))
    return dict(tokens=tokens, frozen_gate_weight=frozen_gate_weight, frozen_up_weight=frozen_up_weight, frozen_down_weight=frozen_down_weight, adapter_down_weight=adapter_down_weight, adapter_up_weight=adapter_up_weight, routes=routes, route_gate_weights=route_gate_weights, output_gradient=output_gradient)


def rounded(values):
    return lax.optimization_barrier(values.astype(jnp.bfloat16)).astype(jnp.float32)


def reference(tokens, frozen_gate_weight, frozen_up_weight, frozen_down_weight, adapter_down_weight, adapter_up_weight, routes, route_gate_weights, output_gradient):
    width_part = MODEL_WIDTH // N_TENSOR
    hidden_part = FF // N_EXPERT

    def gate_block(index, carry):
        first_col = (jnp.asarray(index) * width_part).astype(jnp.int32)
        block_rows = lax.dynamic_slice_in_dim(tokens, first_col, width_part, 1)
        gate_rows = lax.dynamic_slice_in_dim(frozen_gate_weight, first_col, width_part, 0)
        up_rows = lax.dynamic_slice_in_dim(frozen_up_weight, first_col, width_part, 0)
        gate_term = rounded(jnp.dot(block_rows, gate_rows, preferred_element_type=jnp.float32))
        up_term = rounded(jnp.dot(block_rows, up_rows, preferred_element_type=jnp.float32))
        return (carry[0] + gate_term, carry[1] + up_term)

    zero_hidden = jnp.zeros((TOKENS, FF), jnp.float32)
    gate_sum, up_sum = lax.fori_loop(0, N_TENSOR, gate_block, (zero_hidden, zero_hidden))
    hidden = (jax.nn.silu(gate_sum) * up_sum).astype(jnp.bfloat16)

    def down_block(index, carry):
        first_col = (jnp.asarray(index) * hidden_part).astype(jnp.int32)
        block_cols = lax.dynamic_slice_in_dim(hidden, first_col, hidden_part, 1)
        down_rows = lax.dynamic_slice_in_dim(frozen_down_weight, first_col, hidden_part, 0)
        return carry + rounded(jnp.dot(block_cols, down_rows, preferred_element_type=jnp.float32))

    base_out = lax.fori_loop(0, N_EXPERT, down_block, jnp.zeros((TOKENS, MODEL_WIDTH), jnp.float32))

    route_ids = routes.reshape(-1)
    gate_flat = route_gate_weights.reshape(-1)
    capacity = MOST * N_EXPERT

    def per_expert(adapter_sum, expert_slot):
        hits = route_ids == expert_slot
        total_hits = jnp.sum(hits.astype(jnp.int32))
        picks = jnp.nonzero(hits, size=capacity, fill_value=0)[0].astype(jnp.int32)
        valid = jnp.arange(capacity, dtype=jnp.int32) < total_hits
        token_index = (picks // 2).astype(jnp.int32)
        weights = jnp.where(valid, gate_flat[picks], jnp.float32(0.0))
        inputs = jnp.where(valid[:, None], tokens[token_index], jnp.zeros((), jnp.bfloat16))
        down_matrix = adapter_down_weight[expert_slot]
        up_matrix = adapter_up_weight[expert_slot]
        rank_activations = jnp.dot(inputs, down_matrix, preferred_element_type=jnp.float32).astype(jnp.bfloat16)
        expert_out = jnp.dot(rank_activations, up_matrix, preferred_element_type=jnp.float32).astype(jnp.bfloat16)
        adapter_sum = adapter_sum.at[token_index].add(weights[:, None] * expert_out.astype(jnp.float32))
        scaled = (weights[:, None] * output_gradient[token_index].astype(jnp.float32)).astype(jnp.bfloat16)
        grad_b = jnp.dot(rank_activations.T, scaled, preferred_element_type=jnp.float32).astype(jnp.bfloat16)
        back_low = jnp.dot(scaled, up_matrix.T, preferred_element_type=jnp.float32).astype(jnp.bfloat16)
        grad_a = jnp.dot(inputs.T, back_low, preferred_element_type=jnp.float32).astype(jnp.bfloat16)
        return adapter_sum, (grad_a, grad_b)

    adapter_sum, (grad_down, grad_up) = lax.scan(per_expert, jnp.zeros((TOKENS, MODEL_WIDTH), jnp.float32), jnp.arange(EXPERT_COUNT, dtype=jnp.int32))
    ffn_out = (base_out + adapter_sum).astype(jnp.bfloat16)
    return ffn_out, grad_down, grad_up
```

```python
import jax
import jax.numpy as jnp
from jax import lax
from jax.sharding import PartitionSpec as P

F32 = jnp.float32
BF16 = jnp.bfloat16


def activate(gate_part, up_part):
    return (jax.nn.silu(gate_part) * up_part).astype(BF16)


def frozen_layer(shard_rows, gate_weight, up_weight, down_weight):
    hidden_width = gate_weight.shape[1]
    gate_part = jnp.dot(shard_rows, gate_weight, preferred_element_type=F32).astype(BF16)
    up_part = jnp.dot(shard_rows, up_weight, preferred_element_type=F32).astype(BF16)
    summed = lax.psum_scatter(
        jnp.concatenate([gate_part, up_part], axis=1), "tensor", scatter_dimension=0, tiled=True
    ).astype(F32)
    hidden = activate(summed[:, :hidden_width], summed[:, hidden_width:])
    hidden_all = lax.all_gather(hidden, "tensor", axis=0, tiled=True)
    return jnp.dot(hidden_all, down_weight, preferred_element_type=F32)


def per_device(
    tokens,
    frozen_gate_weight,
    frozen_up_weight,
    frozen_down_weight,
    adapter_down_weight,
    adapter_up_weight,
    routes,
    route_gate_weights,
    output_gradient,
):
    n_expert = lax.axis_size("expert")
    tok_count, width_part = tokens.shape
    resident = adapter_down_weight.shape[0]
    most_slots = max(2, 4 * tok_count // (resident * n_expert))
    capacity = most_slots * n_expert
    total = tok_count * n_expert

    shard_rows = lax.all_gather(tokens, "expert", axis=0, tiled=True)
    meta = jnp.concatenate([routes.T.astype(F32), route_gate_weights.T], axis=0)
    meta_all = lax.all_gather(meta, "expert", axis=1, tiled=True)
    grad_rows = lax.all_gather(output_gradient, "expert", axis=0, tiled=True)

    local = (lax.axis_index("expert") * resident + jnp.arange(resident)).astype(F32)
    hit_0 = meta_all[0][None, :] == local[:, None]
    hit_1 = meta_all[1][None, :] == local[:, None]
    member = hit_0 | hit_1
    weight = jnp.where(hit_0, meta_all[2][None, :], 0.0) + jnp.where(
        hit_1, meta_all[3][None, :], 0.0
    )
    span = jnp.arange(tok_count)
    before = (span[:, None] < span[None, :]).astype(BF16)
    rank = jnp.dot(
        member.astype(BF16).reshape(resident * n_expert, tok_count),
        before,
        preferred_element_type=F32,
    ).reshape(resident, total)
    base_slot = (jnp.arange(total) // tok_count * most_slots).astype(F32)
    slot = jnp.where(member, rank + base_slot[None, :], -1.0)
    select = slot[:, None, :] == jnp.arange(capacity, dtype=F32)[None, :, None]
    slot_weight = jnp.sum(jnp.where(select, weight[:, None, :], 0.0), axis=2)
    pick = select.astype(BF16).reshape(resident * capacity, total)

    inputs = jnp.dot(pick, shard_rows, preferred_element_type=F32).astype(BF16)
    inputs = inputs.reshape(resident, capacity, width_part)
    cotangents = jnp.dot(pick, grad_rows, preferred_element_type=F32)
    scaled = (slot_weight[:, :, None] * cotangents.reshape(resident, capacity, width_part)).astype(
        BF16
    )
    low_part = jnp.einsum(
        "ecw,ewr->ecr", inputs, adapter_down_weight, preferred_element_type=F32
    ).astype(BF16)
    back_part = jnp.einsum(
        "ecw,erw->ecr", scaled, adapter_up_weight, preferred_element_type=F32
    ).astype(BF16)
    both = lax.psum(jnp.concatenate([low_part, back_part], axis=2), "tensor")
    rank_width = low_part.shape[2]
    low, back = both[:, :, :rank_width], both[:, :, rank_width:]
    grad_up = jnp.einsum("ecr,ecw->erw", low, scaled, preferred_element_type=F32).astype(BF16)
    grad_down = jnp.einsum("ecw,ecr->ewr", inputs, back, preferred_element_type=F32).astype(BF16)
    rows = jnp.einsum("ecr,erw->ecw", low, adapter_up_weight, preferred_element_type=F32)
    rows = (slot_weight[:, :, None] * rows).astype(BF16).reshape(resident * capacity, width_part)
    adapter_part = lax.dot_general(
        pick, rows, (((0,), (0,)), ((), ())), preferred_element_type=F32
    )

    base_part = frozen_layer(
        shard_rows, frozen_gate_weight, frozen_up_weight, frozen_down_weight
    )
    ffn_out = lax.psum_scatter(
        (base_part + adapter_part).astype(BF16), "expert", scatter_dimension=0, tiled=True
    )
    return (ffn_out, grad_down, grad_up)


def solution(mesh):
    placed = (
        P("expert", "tensor"),
        P("tensor", "expert"),
        P("tensor", "expert"),
        P("expert", "tensor"),
        P("expert", "tensor", None),
        P("expert", None, "tensor"),
        P("expert", None),
        P("expert", None),
        P("expert", "tensor"),
    )
    return jax.shard_map(
        per_device,
        mesh=mesh,
        in_specs=placed,
        out_specs=(P("expert", "tensor"), P("expert", "tensor", None), P("expert", None, "tensor")),
        check_vma=False,
    )
```

```python
import functools

import jax
import jax.numpy as jnp
from jax import lax
from jax.experimental import pallas as pl
from jax.experimental.pallas import tpu as pltpu
from jax.sharding import PartitionSpec as P

F32 = jnp.float32
BF16 = jnp.bfloat16


def activate(gate_part, up_part):
    return (jax.nn.silu(gate_part) * up_part).astype(BF16)


def place():
    me = lax.axis_index("expert")
    z, x = me // 2, me % 2
    return me, z, x, z * 2 + 1 - x, [lax.rem(z + k, 4) for k in range(4)]


def send(src, dst, send_sem, recv_sem, peer):
    return pltpu.make_async_remote_copy(
        src_ref=src, dst_ref=dst, send_sem=send_sem, recv_sem=recv_sem,
        device_id={"expert": peer}, device_id_type=pl.DeviceIdType.MESH,
    )


def greet(x, partner, ahead):
    barrier = pltpu.get_barrier_semaphore()
    for peer in [partner] + [ahead[k] * 2 + x for k in (1, 2, 3)]:
        pl.semaphore_signal(
            barrier, inc=1, device_id={"expert": peer}, device_id_type=pl.DeviceIdType.MESH
        )
    pl.semaphore_wait(barrier, 4)


def block(ref, index, rows):
    return ref.at[pl.ds(pl.multiple_of(index * rows, rows), rows)]


def gather_kernel(count, *refs):
    sources, outs = refs[:count], refs[count:2 * count]
    own_sem, z_send, z_recv, x_send, x_recv = refs[2 * count:]
    me, z, x, partner, ahead = place()
    greet(x, partner, ahead)
    owns, sent = [], []
    for a in range(count):
        rows = sources[a].shape[0]
        own = pltpu.make_async_copy(sources[a], block(outs[a], me, rows), own_sem.at[a])
        own.start()
        owns.append(own)
        for k in (1, 2, 3):
            i = 4 * a + k
            copy = send(sources[a], block(outs[a], me, rows), z_send.at[i], z_recv.at[i],
                        ahead[k] * 2 + x)
            copy.start()
            sent.append(copy)
        copy = send(sources[a], block(outs[a], me, rows), x_send.at[4 * a], x_recv.at[4 * a],
                    partner)
        copy.start()
        sent.append(copy)
    for k in (1, 2, 3):
        origin = ahead[4 - k] * 2
        for a in range(count):
            rows = sources[a].shape[0]
            i = 4 * a + k
            landed = block(outs[a], origin + x, rows)
            send(sources[a], landed, z_send.at[i], z_recv.at[i], partner).wait_recv()
            copy = send(landed, landed, x_send.at[i], x_recv.at[i], partner)
            copy.start()
            sent.append(copy)
    for k in range(4):
        origin = ahead[(4 - k) % 4] * 2 + 1 - x
        for a in range(count):
            rows = sources[a].shape[0]
            i = 4 * a + k
            send(sources[a], block(outs[a], origin, rows), x_send.at[i], x_recv.at[i],
                 partner).wait_recv()
    for copy in sent:
        copy.wait_send()
    for own in owns:
        own.wait()


def gather_rows(arrays, collective):
    count = len(arrays)
    vmem = pl.BlockSpec(memory_space=pltpu.VMEM)
    return pl.pallas_call(
        functools.partial(gather_kernel, count),
        out_shape=[jax.ShapeDtypeStruct((8 * a.shape[0], a.shape[1]), a.dtype) for a in arrays],
        in_specs=[vmem] * count,
        out_specs=[vmem] * count,
        scratch_shapes=[pltpu.SemaphoreType.DMA((count,))]
        + [pltpu.SemaphoreType.DMA((4 * count,))] * 4,
        compiler_params=pltpu.CompilerParams(
            collective_id=collective, has_side_effects=True, vmem_limit_bytes=16 << 20
        ),
    )(*arrays)


def scatter_kernel(part, out, x_buf, sums, z_buf, x_send, x_recv, z_send, z_recv):
    me, z, x, partner, ahead = place()
    rows = out.shape[0]
    greet(x, partner, ahead)
    across, along = {}, []
    for k in (2, 1, 3, 0):
        across[k] = send(block(part, ahead[k] * 2 + 1 - x, rows), x_buf.at[k], x_send.at[k],
                         x_recv.at[k], partner)
        across[k].start()
    for k in (2, 1, 3):
        across[k].wait_recv()
        mine = part[pl.ds(pl.multiple_of((ahead[k] * 2 + x) * rows, rows), rows), :]
        sums[k - 1] = (mine.astype(F32) + x_buf[k].astype(F32)).astype(BF16)
        copy = send(sums.at[k - 1], z_buf.at[k - 1], z_send.at[k - 1], z_recv.at[k - 1],
                    ahead[k] * 2 + x)
        copy.start()
        along.append(copy)
    across[0].wait_recv()
    for copy in along:
        copy.wait_recv()
    mine = part[pl.ds(pl.multiple_of(me * rows, rows), rows), :]
    total = mine.astype(F32) + x_buf[0].astype(F32)
    for k in range(3):
        total += z_buf[k].astype(F32)
    out[...] = total.astype(BF16)
    for k in range(4):
        across[k].wait_send()
    for copy in along:
        copy.wait_send()


def scatter_rows(part, collective):
    rows, width = part.shape[0] // 8, part.shape[1]
    vmem = pl.BlockSpec(memory_space=pltpu.VMEM)
    return pl.pallas_call(
        scatter_kernel,
        out_shape=jax.ShapeDtypeStruct((rows, width), BF16),
        in_specs=[vmem],
        out_specs=vmem,
        scratch_shapes=[
            pltpu.VMEM((4, rows, width), BF16),
            pltpu.VMEM((3, rows, width), BF16),
            pltpu.VMEM((3, rows, width), BF16),
        ]
        + [pltpu.SemaphoreType.DMA((4,))] * 2
        + [pltpu.SemaphoreType.DMA((3,))] * 2,
        compiler_params=pltpu.CompilerParams(
            collective_id=collective, has_side_effects=True, vmem_limit_bytes=16 << 20
        ),
    )(part)


def gate_up_part(shard_rows, gate_weight, up_weight):
    gate_part = jnp.dot(shard_rows, gate_weight, preferred_element_type=F32).astype(BF16)
    up_part = jnp.dot(shard_rows, up_weight, preferred_element_type=F32).astype(BF16)
    return jnp.concatenate([gate_part, up_part], axis=1)


def down_part(summed, down_weight):
    hidden_width = down_weight.shape[0]
    summed = summed.astype(F32)
    hidden = activate(summed[:, :hidden_width], summed[:, hidden_width:])
    hidden_all = lax.all_gather(hidden, "tensor", axis=0, tiled=True)
    return jnp.dot(hidden_all, down_weight, preferred_element_type=F32)


def per_device(
    tokens,
    frozen_gate_weight,
    frozen_up_weight,
    frozen_down_weight,
    adapter_down_weight,
    adapter_up_weight,
    routes,
    route_gate_weights,
    output_gradient,
):
    n_expert = lax.axis_size("expert")
    tok_count, width_part = tokens.shape
    resident = adapter_down_weight.shape[0]
    most_slots = max(2, 4 * tok_count // (resident * n_expert))
    capacity = most_slots * n_expert
    total = tok_count * n_expert

    direct = n_expert == 8 and lax.axis_size("tensor") == 4
    meta = jnp.concatenate([routes.T.astype(F32), route_gate_weights.T], axis=0)
    if direct:
        shard_rows = gather_rows([tokens], 0)[0]
    else:
        shard_rows = lax.all_gather(tokens, "expert", axis=0, tiled=True)
    gate_up = gate_up_part(shard_rows, frozen_gate_weight, frozen_up_weight)
    if direct:
        meta_pad = jnp.pad(meta, ((0, 4), (0, 128 - tok_count)))
        gate_up, output_gradient, meta_pad = lax.optimization_barrier(
            (gate_up, output_gradient, meta_pad)
        )
        summed = lax.psum_scatter(gate_up, "tensor", scatter_dimension=0, tiled=True)
        grad_rows, meta_rows = gather_rows([output_gradient, meta_pad], 1)
        summed, grad_rows, meta_rows = lax.optimization_barrier((summed, grad_rows, meta_rows))
        meta_all = meta_rows.reshape(8, 8, 128)[:, :4, :tok_count].transpose(1, 0, 2)
        meta_all = meta_all.reshape(4, total)
    else:
        summed = lax.psum_scatter(gate_up, "tensor", scatter_dimension=0, tiled=True)
        meta_all = lax.all_gather(meta, "expert", axis=1, tiled=True)
        grad_rows = lax.all_gather(output_gradient, "expert", axis=0, tiled=True)

    local = (lax.axis_index("expert") * resident + jnp.arange(resident)).astype(F32)
    hit_0 = meta_all[0][None, :] == local[:, None]
    hit_1 = meta_all[1][None, :] == local[:, None]
    member = hit_0 | hit_1
    weight = jnp.where(hit_0, meta_all[2][None, :], 0.0) + jnp.where(
        hit_1, meta_all[3][None, :], 0.0
    )
    span = jnp.arange(tok_count)
    before = (span[:, None] < span[None, :]).astype(BF16)
    rank = jnp.dot(
        member.astype(BF16).reshape(resident * n_expert, tok_count),
        before,
        preferred_element_type=F32,
    ).reshape(resident, total)
    base_slot = (jnp.arange(total) // tok_count * most_slots).astype(F32)
    slot = jnp.where(member, rank + base_slot[None, :], -1.0)
    select = slot[:, None, :] == jnp.arange(capacity, dtype=F32)[None, :, None]
    slot_weight = jnp.sum(jnp.where(select, weight[:, None, :], 0.0), axis=2)
    pick = select.astype(BF16).reshape(resident * capacity, total)

    inputs = jnp.dot(pick, shard_rows, preferred_element_type=F32).astype(BF16)
    inputs = inputs.reshape(resident, capacity, width_part)
    cotangents = jnp.dot(pick, grad_rows, preferred_element_type=F32)
    scaled = (slot_weight[:, :, None] * cotangents.reshape(resident, capacity, width_part)).astype(
        BF16
    )
    low_part = jnp.einsum(
        "ecw,ewr->ecr", inputs, adapter_down_weight, preferred_element_type=F32
    ).astype(BF16)
    back_part = jnp.einsum(
        "ecw,erw->ecr", scaled, adapter_up_weight, preferred_element_type=F32
    ).astype(BF16)
    both = lax.psum(jnp.concatenate([low_part, back_part], axis=2), "tensor")
    rank_width = low_part.shape[2]
    low, back = both[:, :, :rank_width], both[:, :, rank_width:]
    grad_up = jnp.einsum("ecr,ecw->erw", low, scaled, preferred_element_type=F32).astype(BF16)
    grad_down = jnp.einsum("ecw,ecr->ewr", inputs, back, preferred_element_type=F32).astype(BF16)
    rows = jnp.einsum("ecr,erw->ecw", low, adapter_up_weight, preferred_element_type=F32)
    rows = (slot_weight[:, :, None] * rows).astype(BF16).reshape(resident * capacity, width_part)
    adapter_part = lax.dot_general(
        pick, rows, (((0,), (0,)), ((), ())), preferred_element_type=F32
    )

    part = (down_part(summed, frozen_down_weight) + adapter_part).astype(BF16)
    if direct:
        ffn_out = scatter_rows(part, 2)
    else:
        ffn_out = lax.psum_scatter(part, "expert", scatter_dimension=0, tiled=True)
    return (ffn_out, grad_down, grad_up)


def solution(mesh):
    placed = (
        P("expert", "tensor"),
        P("tensor", "expert"),
        P("tensor", "expert"),
        P("expert", "tensor"),
        P("expert", "tensor", None),
        P("expert", None, "tensor"),
        P("expert", None),
        P("expert", None),
        P("expert", "tensor"),
    )
    return jax.shard_map(
        per_device,
        mesh=mesh,
        in_specs=placed,
        out_specs=(P("expert", "tensor"), P("expert", "tensor", None), P("expert", None, "tensor")),
        check_vma=False,
    )
```
